256 devices in a mesh: row: 8 (over z_hi, core), col: 32 (over x, y, z_lo).
Axes of the slice: x: 4, y: 4, z: 8 (z_hi: 4, z_lo: 2; z = z_hi * 2 + z_lo), core: 2. Of those that a mesh axis runs over, the one named last changes fastest.
Arguments:
- object_re: float32 [2048, 8192], P('row', 'col'), may hold values from -6 to 6
- object_im: float32 [2048, 8192], P('row', 'col'), may hold values from -6 to 6
- probe_re: float32 [256, 256], replicated, may hold values from -4 to 4
- probe_im: float32 [256, 256], replicated, may hold values from -4 to 4
- intensity: float32 [8, 32, 4, 256, 256], P('row', 'col'), may hold values from 0.05 to 4
- offsets: int32 [8, 32, 4, 2], P('row', 'col'), may hold values from 48 to 208
- counts: int32 [8, 32], P('row', 'col'), may hold values from 2 to 4
Outputs:
- final_re: float32 [2048, 8192], P('row', 'col')
- final_im: float32 [2048, 8192], P('row', 'col')
The draws below stay inside these ranges and needn't reach their ends.
All inputs are finite; a program needn't handle non-finite values.
Results may differ from the reference program's by a relative error of at most 0.00024.
Values sent between devices are 32-bit elements; how exact they have to be, the bound alone decides.
No kernel may reach another device: no remote copies, remote signals or barrier semaphores. Data moves between devices by JAX's collectives and lax.ppermute only.
A program may use at most 64 MiB of HBM per device.

```python
import math
import jax
import jax.numpy as jnp
from jax import lax

W = 256
ITERS = 2
TR = 256
TC = 256
STEP = 128
POS = 4
GRID_R = 8
GRID_C = 32
NR = 2048
NC = 8192


def draw_offsets(key, part):
    across = TC // STEP
    jitter_most = STEP // 8
    serial = jnp.arange(POS).astype(jnp.int32)
    base_rows = serial // across * STEP + STEP // 2
    base_cols = serial % across * STEP + STEP // 2
    base = jnp.stack([base_rows, base_cols], axis=1).astype(jnp.int32)
    jitter = jax.random.randint(key, (GRID_R, GRID_C, POS, 2), -jitter_most, jitter_most + 1)
    jitter = jitter.at[0, 0, 0].set(jnp.full((2,), -jitter_most, jnp.int32))
    jitter = jitter.at[GRID_R - 1, GRID_C - 1, POS - 1].set(jnp.full((2,), jitter_most, jnp.int32))
    return (base[None, None] + jitter).astype(jnp.int32)


def draw_counts(key, part):
    values = jax.random.randint(key, (GRID_R, GRID_C), POS // 2, POS + 1)
    values = values.at[0, 0].set(POS // 2)
    values = values.at[GRID_R - 1, GRID_C - 1].set(POS)
    return values.astype(jnp.int32)


def levels(key, shape, cuts, low, high):
    loudness = 1.0
    for position, shards_of in cuts:
        steps = jax.random.uniform(jax.random.fold_in(jax.random.fold_in(key, 6), position), (shards_of,), jnp.float32, low / len(cuts), high / len(cuts))
        loudness = loudness * jnp.repeat(jnp.exp(steps), shape[position] // shards_of).reshape((-1,) + (1,) * (len(shape) - 1 - position))
    return loudness


def bell_draw(stream_key, dims, width, reach, pieces=(), kind=jnp.bfloat16):
    values = width * jax.random.normal(stream_key, dims, jnp.float32)
    if pieces:
        values = values * levels(stream_key, dims, pieces, -0.22, 0.18)
    return jnp.clip(values, -reach, reach).astype(kind)


def setup_inputs(seed: int = 0) -> dict:
    keys = jax.random.split(jax.random.key(seed), 8)
    object_re = bell_draw(keys[0], (NR, NC), 1.0, 6.0, ((0, 8), (1, 32)), jnp.float32)
    object_im = bell_draw(keys[1], (NR, NC), 1.0, 6.0, ((0, 8), (1, 32)), jnp.float32)
    probe_re = bell_draw(keys[2], (W, W), 0.7, 4.0, (), jnp.float32)
    probe_im = bell_draw(keys[3], (W, W), 0.7, 4.0, (), jnp.float32)
    intensity = jnp.clip(jnp.exp(math.log(4.0) - 4.3820266 * jax.random.uniform(keys[4], (GRID_R, GRID_C, POS, W, W), jnp.float32) ** levels(keys[4], (GRID_R, GRID_C, POS, W, W), ((0, 8), (1, 32)), -0.2, 0.2)), 0.05, 4.0)
    offsets = draw_offsets(jax.random.fold_in(keys[7], 71), 0)
    counts = draw_counts(jax.random.fold_in(keys[7], 71), 0)
    return dict(object_re=object_re, object_im=object_im, probe_re=probe_re, probe_im=probe_im, intensity=intensity, offsets=offsets, counts=counts)


smoothing = 0.01
step_size = 0.25

def reference(object_re, object_im, probe_re, probe_im, intensity, offsets, counts):
    margin = W // 2
    probe = lax.complex(probe_re, probe_im)
    total_positions = GRID_R * GRID_C * POS
    serial = jnp.arange(total_positions).astype(jnp.int32)
    tile_row = (serial // (GRID_C * POS)).astype(jnp.int32)
    tile_col = (serial // POS % GRID_C).astype(jnp.int32)
    slot = (serial % POS).astype(jnp.int32)
    flat_offsets = offsets.reshape(total_positions, 2).astype(jnp.int32)
    flat_counts = counts.reshape(GRID_R * GRID_C)
    weights = (slot < flat_counts[serial // POS]).astype(object_re.dtype)
    start_row = (tile_row * TR + flat_offsets[:, 0]).astype(jnp.int32)
    start_col = (tile_col * TC + flat_offsets[:, 1]).astype(jnp.int32)
    measured = intensity.reshape(total_positions, W, W)
    real_part, imag_part = (object_re, object_im)
    for sweep in range(ITERS):
        padded = jnp.pad(jnp.stack([real_part, imag_part]), ((0, 0), (margin, margin), (margin, margin)))

        def visit(gradient, scan_entry):
            leading_row, leading_column, measured_amplitude, update_weight = scan_entry
            corner = (jnp.zeros((), jnp.int32), leading_row, leading_column)
            patch = lax.dynamic_slice(padded, corner, (2, W, W))
            wave = lax.complex(patch[0], patch[1]) * probe
            farfield_wave = jnp.fft.fft2(wave, norm='ortho')
            wave_magnitude = jnp.sqrt(farfield_wave.real * farfield_wave.real + farfield_wave.imag * farfield_wave.imag + smoothing)
            magnitude_error = farfield_wave * (1.0 - jnp.sqrt(measured_amplitude) / wave_magnitude)
            back = jnp.fft.ifft2(magnitude_error, norm='ortho') * jnp.conj(probe)
            term = jnp.stack([back.real, back.imag]) * update_weight
            current = lax.dynamic_slice(gradient, corner, (2, W, W))
            return (lax.dynamic_update_slice(gradient, current + term, corner), None)
        gradient, _ = lax.scan(visit, jnp.zeros_like(padded), (start_row, start_col, measured, weights))
        inner = gradient[:, margin:margin + NR, margin:margin + NC]
        real_part = real_part - step_size * inner[0]
        imag_part = imag_part - step_size * inner[1]
    return (real_part, imag_part)
```

```python
import functools
import math

import jax
import jax.numpy as jnp
import numpy as np
from jax import lax
from jax.experimental import pallas as pl
from jax.experimental.pallas import tpu as pltpu
from jax.sharding import PartitionSpec as P

ITERS = 2

smoothing = 0.01
step_size = 0.25

W = 256
H = 128
REACH = 80
EXT = W + 2 * REACH

VMEM = pl.BlockSpec(memory_space=pltpu.VMEM)
SMEM = pl.BlockSpec(memory_space=pltpu.SMEM)
f32 = jnp.float32
bf16 = jnp.bfloat16


def shape(*dims):
    return jax.ShapeDtypeStruct(dims, f32)


def dft_tables():
    k = np.arange(H)[:, None]
    mats = []
    for odd in (0, 1):
        freq = 2 * np.arange(H)[None, :] + odd
        angle = -2.0 * math.pi * ((k * freq) % W) / W
        c, s = np.cos(angle) / 16.0, np.sin(angle) / 16.0
        mats.append(np.block([[c, s], [-s, c]]))
    mats = [mats[0], mats[1], mats[0].T, mats[1].T]
    out = []
    for m in mats:
        m = m.astype(np.float32)
        hi = m.astype(jnp.bfloat16)
        lo = (m - hi.astype(np.float32)).astype(jnp.bfloat16)
        out.extend([hi, lo])
    return np.stack(out)


def split(x):
    hi = x.astype(bf16)
    lo = (x - hi.astype(f32)).astype(bf16)
    return hi, lo


def dot(a, b):
    return lax.dot_general(a, b, (((1,), (0,)), ((), ())), preferred_element_type=f32)


def right(x, tables, i):
    hi, lo = split(x)
    t_hi, t_lo = tables[2 * i], tables[2 * i + 1]
    return dot(
        jnp.concatenate([hi, lo, hi], axis=1), jnp.concatenate([t_hi, t_hi, t_lo], axis=0)
    )


def left(tables, i, x):
    hi, lo = split(x)
    t_hi, t_lo = tables[2 * i], tables[2 * i + 1]
    return dot(
        jnp.concatenate([t_hi, t_hi, t_lo], axis=1), jnp.concatenate([hi, lo, hi], axis=0)
    )


def cat(a, b, axis):
    return jnp.concatenate([a, b], axis=axis)


def roots_kernel(intensity, out):
    row = lax.broadcasted_iota(jnp.int32, (W, W), 0)
    col = lax.broadcasted_iota(jnp.int32, (W, W), 1)
    source = jnp.where(col < H, 2 * col, 2 * (col - H) + 1)
    perm = jnp.where(row == source, 1.0, 0.0).astype(bf16)
    perm3 = jnp.concatenate([perm, perm, perm], axis=0)
    for p in range(out.shape[0]):
        x = jnp.sqrt(intensity[p])
        hi = x.astype(bf16)
        rest = x - hi.astype(f32)
        mid = rest.astype(bf16)
        lo = (rest - mid.astype(f32)).astype(bf16)
        y = dot(jnp.concatenate([hi, mid, lo], axis=1), perm3)
        y = y.reshape(H, 2, W)
        out[p, pl.ds(0, H), :] = y[:, 0, :]
        out[p, pl.ds(H, H), :] = y[:, 1, :]


def columns_kernel(re, im, to_left, to_right):
    for comp, x in enumerate((re, im)):
        to_left[comp] = x[:, 0:H].T[:REACH]
        to_right[comp] = x[:, H:W].T[H - REACH :]


def fill_sides(mid, from_left, from_right):
    blank = jnp.zeros((H - REACH, W), f32)
    for comp in range(2):
        mid[comp, 0] = jnp.concatenate([blank, from_left[comp]], axis=0).T
        mid[comp, 3] = jnp.concatenate([from_right[comp], blank], axis=0).T


def widen_kernel(re, im, from_left, from_right, mid, top, bottom):
    for comp, x in enumerate((re, im)):
        mid[comp, 1] = x[:, 0:H]
        mid[comp, 2] = x[:, H:W]
    fill_sides(mid, from_left, from_right)
    top[...] = mid[:, :, 0:REACH, :]
    bottom[...] = mid[:, :, W - REACH : W, :]


def gradient_kernel(
    offsets, counts, from_top, mid, from_bottom, roots, probe_re, probe_im, tables,
    to_top, centre, to_bottom, ext, acc,
):
    ext[:, :, 0:REACH, :] = from_top[...]
    ext[:, :, REACH : REACH + W, :] = mid[...]
    ext[:, :, REACH + W :, :] = from_bottom[...]
    acc[...] = jnp.zeros(acc.shape, f32)
    lane = lax.broadcasted_iota(jnp.int32, (W, H), 1)

    def position(p, carry):
        row = offsets[p, 0] - (H - REACH)
        base = lax.rem(p, 2)
        shift = offsets[p, 1] - H * base
        rows = pl.ds(row, W)
        o = []
        for comp in range(2):
            rolled = [pltpu.roll(ext[comp, base + j, rows, :], H - shift, 1) for j in range(3)]
            o.append([jnp.where(lane < H - shift, rolled[j], rolled[j + 1]) for j in range(2)])
        w_re, w_im = [], []
        for j in range(2):
            p_re, p_im = probe_re[:, j * H : (j + 1) * H], probe_im[:, j * H : (j + 1) * H]
            w_re.append(o[0][j] * p_re - o[1][j] * p_im)
            w_im.append(o[0][j] * p_im + o[1][j] * p_re)
        e = right(cat(w_re[0] + w_re[1], w_im[0] + w_im[1], 1), tables, 0)
        d = right(cat(w_re[0] - w_re[1], w_im[0] - w_im[1], 1), tables, 1)
        h_re = cat(e[:, :H], d[:, :H], 1)
        h_im = cat(e[:, H:], d[:, H:], 1)
        far_e = left(tables, 2, cat(h_re[:H] + h_re[H:], h_im[:H] + h_im[H:], 0))
        far_d = left(tables, 3, cat(h_re[:H] - h_re[H:], h_im[:H] - h_im[H:], 0))

        def residual(far, root):
            power = far[:H] * far[:H] + far[H:] * far[H:] + smoothing
            factor = 1.0 - root * lax.rsqrt(power)
            return far * cat(factor, factor, 0)

        a = left(tables, 0, residual(far_e, roots[p, pl.ds(0, H), :]))
        b = left(tables, 1, residual(far_d, roots[p, pl.ds(H, H), :]))
        upper, lower = a + b, a - b
        h_re = cat(upper[:H], lower[:H], 0)
        h_im = cat(upper[H:], lower[H:], 0)
        a = right(cat(h_re[:, :H], h_im[:, :H], 1), tables, 2)
        b = right(cat(h_re[:, H:], h_im[:, H:], 1), tables, 3)
        weight = jnp.where(p < counts[0, 0], 1.0, 0.0).astype(f32)
        g_re, g_im = [], []
        for j, x in enumerate((a + b, a - b)):
            p_re, p_im = probe_re[:, j * H : (j + 1) * H], probe_im[:, j * H : (j + 1) * H]
            p_re, p_im = p_re * weight, p_im * weight
            g_re.append(x[:, :H] * p_re + x[:, H:] * p_im)
            g_im.append(x[:, H:] * p_re - x[:, :H] * p_im)
        for comp, g in enumerate((g_re, g_im)):
            r = [pltpu.roll(g[j], shift, 1) for j in range(2)]
            acc[comp, base, rows, :] += jnp.where(lane >= shift, r[0], 0.0)
            acc[comp, base + 1, rows, :] += jnp.where(lane >= shift, r[1], r[0])
            acc[comp, base + 2, rows, :] += jnp.where(lane < shift, r[1], 0.0)
        return carry

    lax.fori_loop(0, roots.shape[0], position, 0)
    to_top[...] = acc[:, :, 0:REACH, :]
    centre[...] = acc[:, :, REACH : REACH + W, :]
    to_bottom[...] = acc[:, :, REACH + W :, :]


def add_rows(centre, from_top, from_bottom, total):
    total[...] = centre[...]
    total[:, :, 0:REACH, :] += from_top[...]
    total[:, :, W - REACH : W, :] += from_bottom[...]


def rows_kernel(reach, centre, from_top, from_bottom, total, to_left, to_right):
    add_rows(centre, from_top, from_bottom, total)
    for comp in range(2):
        to_left[comp, 0:REACH] = total[comp, 0].T[H - REACH :]
        to_right[comp, reach - REACH :] = total[comp, 3].T[:REACH]
        if reach > REACH:
            to_left[comp, REACH:] = total[comp, 1].T[:REACH]
            to_right[comp, 0:REACH] = total[comp, 2].T[H - REACH :]


def step_kernel(edges, mid, total, from_left, from_right, out, top, bottom):
    blank = jnp.zeros((H - REACH, W), f32)
    keep_left = jnp.where(edges[0] != 0, 0.0, 1.0).astype(f32)
    keep_right = jnp.where(edges[1] != 0, 0.0, 1.0).astype(f32)
    for comp in range(2):
        add = [
            cat(blank, from_left[comp, 0:REACH], 0).T,
            cat(from_left[comp, REACH:], blank, 0).T,
            cat(blank, from_right[comp, 0:REACH], 0).T,
            cat(from_right[comp, REACH:], blank, 0).T,
        ]
        keep = [keep_left, None, None, keep_right]
        for j in range(4):
            value = mid[comp, j] - step_size * (total[comp, j] + add[j])
            out[comp, j] = value if keep[j] is None else value * keep[j]
    top[...] = out[:, :, 0:REACH, :]
    bottom[...] = out[:, :, W - REACH : W, :]


def final_kernel(mid, total, from_left, from_right, out_re, out_im):
    blank = jnp.zeros((H - REACH, W), f32)
    for comp, out in enumerate((out_re, out_im)):
        add = [
            cat(from_left[comp], blank, 0).T,
            cat(blank, from_right[comp], 0).T,
        ]
        for j in range(2):
            value = mid[comp, j + 1] - step_size * (total[comp, j + 1] + add[j])
            out[:, j * H : (j + 1) * H] = value


def call(kernel, specs, out_shape, *args, scratch=(), flops=0, read=0):
    return pl.pallas_call(
        kernel,
        in_specs=specs,
        out_specs=jax.tree.map(lambda _: VMEM, out_shape),
        out_shape=out_shape,
        scratch_shapes=scratch,
        compiler_params=pltpu.CompilerParams(vmem_limit_bytes=48 * 1024 * 1024),
        cost_estimate=pl.CostEstimate(flops=flops, bytes_accessed=read, transcendentals=0),
    )(*args)


def exchange(axis, to_before, to_after):
    size = lax.axis_size(axis)
    up = [(i, i + 1) for i in range(size - 1)]
    down = [(j, i) for i, j in up]
    return lax.ppermute(to_after, axis, up), lax.ppermute(to_before, axis, down)


def shards(object_re, object_im, probe_re, probe_im, intensity, offsets, counts):
    slots = intensity.shape[2]
    placed = offsets[0, 0]
    tables = jnp.asarray(dft_tables())
    column = lax.axis_index("col")
    last = lax.axis_size("col") - 1
    edges = jnp.stack([column == 0, column == last]).astype(jnp.int32)

    strip = shape(2, REACH, W)
    wide = shape(2, 2 * REACH, W)
    rows = shape(2, 4, REACH, H)
    full = shape(2, 4, W, H)

    to_left, to_right = call(columns_kernel, [VMEM] * 2, (strip, strip), object_re, object_im, read=1 << 20)
    from_left, from_right = exchange("col", to_left, to_right)
    roots = call(roots_kernel, [VMEM], shape(slots, W, W), intensity[0, 0], flops=1 << 29, read=1 << 21)
    mid, top, bottom = call(
        widen_kernel, [VMEM] * 4, (full, rows, rows), object_re, object_im, from_left, from_right, read=1 << 21
    )
    for sweep in range(ITERS):
        from_top, from_bottom = exchange("row", top, bottom)
        to_top, centre, to_bottom = call(
            gradient_kernel,
            [SMEM, SMEM] + [VMEM] * 7,
            (rows, full, rows),
            placed, counts, from_top, mid, from_bottom, roots, probe_re, probe_im, tables,
            scratch=[pltpu.VMEM((2, 4, EXT, H), f32)] * 2,
            flops=1 << 32,
            read=1 << 23,
        )
        from_top, from_bottom = exchange("row", to_top, to_bottom)
        final = sweep == ITERS - 1
        reach = REACH if final else 2 * REACH
        strips = strip if final else wide
        total, to_left, to_right = call(
            functools.partial(rows_kernel, reach),
            [VMEM] * 3,
            (full, strips, strips),
            centre, from_top, from_bottom,
            read=1 << 21,
        )
        from_left, from_right = exchange("col", to_left, to_right)
        if final:
            tile = shape(W, W)
            return call(
                final_kernel, [VMEM] * 4, (tile, tile), mid, total, from_left, from_right, read=1 << 21
            )
        mid, top, bottom = call(
            step_kernel, [SMEM] + [VMEM] * 4, (full, rows, rows),
            edges, mid, total, from_left, from_right, read=1 << 21,
        )


def solution(mesh):
    return jax.shard_map(
        shards,
        mesh=mesh,
        in_specs=(
            P("row", "col"),
            P("row", "col"),
            P(),
            P(),
            P("row", "col", None, None, None),
            P("row", "col", None, None),
            P("row", "col"),
        ),
        out_specs=(P("row", "col"), P("row", "col")),
        check_vma=False,
    )
```

```python
import math

import jax
import jax.numpy as jnp
import numpy as np
from jax import lax
from jax.experimental import pallas as pl
from jax.experimental.pallas import tpu as pltpu
from jax.sharding import PartitionSpec as P

ITERS = 2

smoothing = 0.01
step_size = 0.25

W = 256
H = 128
REACH = 80
PART = W // 2 + REACH
HALF = PART + REACH

VMEM = pl.BlockSpec(memory_space=pltpu.VMEM)
SMEM = pl.BlockSpec(memory_space=pltpu.SMEM)
f32 = jnp.float32
bf16 = jnp.bfloat16


def shape(*dims):
    return jax.ShapeDtypeStruct(dims, f32)


def dft_tables():
    k = np.arange(H)[:, None]
    mats = []
    for odd in (0, 1):
        freq = 2 * np.arange(H)[None, :] + odd
        angle = -2.0 * math.pi * ((k * freq) % W) / W
        c, s = np.cos(angle) / 16.0, np.sin(angle) / 16.0
        mats.append(np.block([[c, s], [-s, c]]))
    mats = [mats[0], mats[1], mats[0].T, mats[1].T]
    out = []
    for m in mats:
        m = m.astype(np.float32)
        hi = m.astype(jnp.bfloat16)
        lo = (m - hi.astype(np.float32)).astype(jnp.bfloat16)
        out.extend([hi, lo])
    return np.stack(out)


def split(x):
    hi = x.astype(bf16)
    lo = (x - hi.astype(f32)).astype(bf16)
    return hi, lo


def dot(a, b):
    return lax.dot_general(a, b, (((1,), (0,)), ((), ())), preferred_element_type=f32)


def right(x, tables, i):
    hi, lo = split(x)
    t_hi, t_lo = tables[2 * i], tables[2 * i + 1]
    return dot(
        jnp.concatenate([hi, lo, hi], axis=1), jnp.concatenate([t_hi, t_hi, t_lo], axis=0)
    )


def left(tables, i, x):
    hi, lo = split(x)
    t_hi, t_lo = tables[2 * i], tables[2 * i + 1]
    return dot(
        jnp.concatenate([t_hi, t_hi, t_lo], axis=1), jnp.concatenate([hi, lo, hi], axis=0)
    )


def cat(a, b, axis):
    return jnp.concatenate([a, b], axis=axis)


def roots_kernel(intensity, out):
    row = lax.broadcasted_iota(jnp.int32, (W, W), 0)
    col = lax.broadcasted_iota(jnp.int32, (W, W), 1)
    source = jnp.where(col < H, 2 * col, 2 * (col - H) + 1)
    perm = jnp.where(row == source, 1.0, 0.0).astype(bf16)
    perm3 = jnp.concatenate([perm, perm, perm], axis=0)
    for p in range(out.shape[0]):
        x = jnp.sqrt(intensity[p])
        hi = x.astype(bf16)
        rest = x - hi.astype(f32)
        mid = rest.astype(bf16)
        lo = (rest - mid.astype(f32)).astype(bf16)
        y = dot(jnp.concatenate([hi, mid, lo], axis=1), perm3)
        y = y.reshape(H, 2, W)
        out[p, pl.ds(0, H), :] = y[:, 0, :]
        out[p, pl.ds(H, H), :] = y[:, 1, :]


def rows_at(start, size):
    return pl.ds(pl.multiple_of(start, 8), size)


def columns_for(flags, left, right, even, odd):
    flip = flags[0] == 1
    for comp in range(2):
        even[comp] = jnp.where(flip, left[comp], right[comp])
        odd[comp] = jnp.where(flip, right[comp], left[comp])


def columns_from(flags, even, odd, comp):
    flip = flags[0] == 1
    return jnp.where(flip, even[comp], odd[comp]), jnp.where(flip, odd[comp], even[comp])


def corners_for(flags, left, right, first, second):
    flip = flags[1] == 1
    for comp in range(2):
        first[comp] = jnp.where(flip, right[comp], left[comp])
        second[comp] = jnp.where(flip, left[comp], right[comp])


def corners_from(flags, first, second, comp):
    flip = flags[1] == 1
    return jnp.where(flip, second[comp], first[comp]), jnp.where(flip, first[comp], second[comp])


def send_object(flags, re, im, even, odd, off, first, second):
    rows = rows_at((W - REACH) * flags[1], REACH)
    left, right, c_left, c_right = [], [], [], []
    for comp, x in enumerate((re, im)):
        left.append(x[:, 0:H].T[:REACH])
        right.append(x[:, H:W].T[H - REACH :])
        c_left.append(x[rows, 0:H])
        c_right.append(x[rows, H:W])
        off[comp, 0] = c_left[comp]
        off[comp, 1] = c_right[comp]
    columns_for(flags, left, right, even, odd)
    corners_for(flags, c_left, c_right, first, second)


def sides_kernel(flags, re, im, even, odd, mid, on):
    blank = jnp.zeros((H - REACH, W), f32)
    for comp, x in enumerate((re, im)):
        from_left, from_right = columns_from(flags, even, odd, comp)
        mid[comp, 0] = cat(blank, from_left, 0).T
        mid[comp, 1] = x[:, 0:H]
        mid[comp, 2] = x[:, H:W]
        mid[comp, 3] = cat(from_right, blank, 0).T
    on[...] = mid[:, :, rows_at((W - REACH) * (1 - flags[1]), REACH), :]


def half_gradient(a, offsets, counts, roots, probe_re, probe_im, tables, ext, acc):
    acc[...] = jnp.zeros(acc.shape, f32)
    lane = lax.broadcasted_iota(jnp.int32, (W, H), 1)

    def position(base, carry):
        p = 2 * a + base
        shift = offsets[p, 1] - H * base
        rows = pl.ds(offsets[p, 0] - (H - REACH) - H * a, W)
        o = []
        for comp in range(2):
            rolled = [pltpu.roll(ext[comp, base + j, rows, :], H - shift, 1) for j in range(3)]
            o.append([jnp.where(lane < H - shift, rolled[j], rolled[j + 1]) for j in range(2)])
        w_re, w_im = [], []
        for j in range(2):
            p_re, p_im = probe_re[:, j * H : (j + 1) * H], probe_im[:, j * H : (j + 1) * H]
            w_re.append(o[0][j] * p_re - o[1][j] * p_im)
            w_im.append(o[0][j] * p_im + o[1][j] * p_re)
        e = right(cat(w_re[0] + w_re[1], w_im[0] + w_im[1], 1), tables, 0)
        d = right(cat(w_re[0] - w_re[1], w_im[0] - w_im[1], 1), tables, 1)
        h_re = cat(e[:, :H], d[:, :H], 1)
        h_im = cat(e[:, H:], d[:, H:], 1)
        far_e = left(tables, 2, cat(h_re[:H] + h_re[H:], h_im[:H] + h_im[H:], 0))
        far_d = left(tables, 3, cat(h_re[:H] - h_re[H:], h_im[:H] - h_im[H:], 0))

        def residual(far, root):
            power = far[:H] * far[:H] + far[H:] * far[H:] + smoothing
            factor = 1.0 - root * lax.rsqrt(power)
            return far * cat(factor, factor, 0)

        x = left(tables, 0, residual(far_e, roots[p, pl.ds(0, H), :]))
        y = left(tables, 1, residual(far_d, roots[p, pl.ds(H, H), :]))
        upper, lower = x + y, x - y
        h_re = cat(upper[:H], lower[:H], 0)
        h_im = cat(upper[H:], lower[H:], 0)
        x = right(cat(h_re[:, :H], h_im[:, :H], 1), tables, 2)
        y = right(cat(h_re[:, H:], h_im[:, H:], 1), tables, 3)
        weight = jnp.where(p < counts[0, 0], 1.0, 0.0).astype(f32)
        g_re, g_im = [], []
        for j, z in enumerate((x + y, x - y)):
            p_re, p_im = probe_re[:, j * H : (j + 1) * H], probe_im[:, j * H : (j + 1) * H]
            p_re, p_im = p_re * weight, p_im * weight
            g_re.append(z[:, :H] * p_re + z[:, H:] * p_im)
            g_im.append(z[:, H:] * p_re - z[:, :H] * p_im)
        for comp, g in enumerate((g_re, g_im)):
            r = [pltpu.roll(g[j], shift, 1) for j in range(2)]
            acc[comp, base, rows, :] += jnp.where(lane >= shift, r[0], 0.0)
            acc[comp, base + 1, rows, :] += jnp.where(lane >= shift, r[1], r[0])
            acc[comp, base + 2, rows, :] += jnp.where(lane < shift, r[1], 0.0)
        return carry

    lax.fori_loop(0, 2, position, 0)


def margin_rows(a):
    return rows_at(PART * a, REACH)


def own_rows(a):
    return rows_at(REACH - REACH * a, PART)


def covered_rows(a):
    return rows_at((W - PART) * a, PART)


def on_kernel(
    flags, offsets, counts, mid, from_on, roots, probe_re, probe_im, tables, part, to_on, ext, acc
):
    a = 1 - flags[1]
    ext[:, :, own_rows(a), :] = mid[:, :, covered_rows(a), :]
    ext[:, :, margin_rows(a), :] = from_on[...]
    half_gradient(a, offsets, counts, roots, probe_re, probe_im, tables, ext, acc)
    part[...] = acc[:, :, own_rows(a), :]
    to_on[...] = acc[:, :, margin_rows(a), :]


def off_kernel(
    flags, offsets, counts, mid, off, first, second, part, from_on, roots, probe_re, probe_im, tables,
    total, to_even, to_odd, to_off, to_first, to_second, ext, acc, centre,
):
    a = flags[1]
    ext[:, :, own_rows(a), :] = mid[:, :, covered_rows(a), :]
    margin = margin_rows(a)
    for comp in range(2):
        left, right = corners_from(flags, first, second, comp)
        ext[comp, 0, margin, :] = left
        ext[comp, 1, margin, :] = off[comp, 0]
        ext[comp, 2, margin, :] = off[comp, 1]
        ext[comp, 3, margin, :] = right
    half_gradient(a, offsets, counts, roots, probe_re, probe_im, tables, ext, acc)
    for j in range(2):
        to_off[:, j] = acc[:, 1 + j, margin, :]
    corners_for(
        flags, [acc[c, 0, margin, :] for c in range(2)], [acc[c, 3, margin, :] for c in range(2)],
        to_first, to_second,
    )
    centre[...] = jnp.zeros(centre.shape, f32)
    centre[:, :, covered_rows(1 - a), :] = part[...]
    centre[:, :, covered_rows(a), :] += acc[:, :, own_rows(a), :]
    centre[:, :, rows_at((W - REACH) * (1 - a), REACH), :] += from_on[...]
    left = [centre[c, 0].T[H - REACH :] for c in range(2)]
    right = [centre[c, 3].T[:REACH] for c in range(2)]
    columns_for(flags, left, right, to_even, to_odd)
    for j in range(2):
        total[:, j] = centre[:, 1 + j]


def step_kernel(flags, re, im, total, even, odd, off, first, second, out_re, out_im, *sends):
    *sends, work = sends
    blank = jnp.zeros((H - REACH, W), f32)
    rows = rows_at((W - REACH) * flags[1], REACH)
    for comp in range(2):
        from_left, from_right = columns_from(flags, even, odd, comp)
        work[comp, 0] = total[comp, 0] + cat(from_left, blank, 0).T
        work[comp, 1] = total[comp, 1] + cat(blank, from_right, 0).T
        corners = corners_from(flags, first, second, comp)
        for j in range(2):
            work[comp, j, rows, :] += off[comp, j] + corners[j]
    for comp, (x, out) in enumerate(((re, out_re), (im, out_im))):
        for j in range(2):
            out[:, j * H : (j + 1) * H] = x[:, j * H : (j + 1) * H] - step_size * work[comp, j]
    if sends:
        send_object(flags, out_re, out_im, *sends)


def call(kernel, scalars, out_shape, *args, scratch=(), flops=0, read=0):
    return pl.pallas_call(
        kernel,
        in_specs=[SMEM] * scalars + [VMEM] * (len(args) - scalars),
        out_specs=jax.tree.map(lambda _: VMEM, out_shape),
        out_shape=out_shape,
        scratch_shapes=scratch,
        compiler_params=pltpu.CompilerParams(vmem_limit_bytes=48 * 1024 * 1024),
        cost_estimate=pl.CostEstimate(flops=flops, bytes_accessed=read, transcendentals=0),
    )(*args)


def swaps(size, bit):
    return [p for i in range(bit, size - 1, 2) for p in ((i, i + 1), (i + 1, i))]


def exchange(even, odd, off, first, second):
    height, width = lax.axis_size("row"), lax.axis_size("col")
    diagonal = ([], [])
    for r in range(1, height - 1, 2):
        for c in range(width):
            for k, d in enumerate((c + 1, c - 1)):
                if 0 <= d < width:
                    diagonal[k].extend([(r * width + c, r * width + width + d), (r * width + width + d, r * width + c)])
    both = ("row", "col")
    moves = (
        (even, "col", swaps(width, 0)),
        (odd, "col", swaps(width, 1)),
        (off, "row", swaps(height, 1)),
        (first, both, diagonal[0]),
        (second, both, diagonal[1]),
    )
    got = []
    for x, axis, pairs in moves:
        got.append(lax.ppermute(x, axis, pairs))
    return got


def shards(object_re, object_im, probe_re, probe_im, intensity, offsets, counts):
    slots = intensity.shape[2]
    placed = offsets[0, 0]
    tables = jnp.asarray(dft_tables())
    flags = jnp.stack([lax.axis_index("col") % 2, lax.axis_index("row") % 2]).astype(jnp.int32)
    on_chip = swaps(lax.axis_size("row"), 0)

    tile = shape(W, W)
    strip = shape(2, REACH, W)
    corner = shape(2, REACH, H)
    sends = (strip, strip, shape(2, 2, REACH, H), corner, corner)
    rows = shape(2, 4, REACH, H)
    full = shape(2, 4, W, H)
    part = shape(2, 4, PART, H)
    halves = [pltpu.VMEM((2, 4, HALF, H), f32)] * 2
    fixed = (probe_re, probe_im, tables)

    re, im = object_re, object_im
    out = call(send_object, 1, sends, flags, re, im, read=1 << 20)
    roots = call(roots_kernel, 0, shape(slots, W, W), intensity[0, 0], flops=1 << 29, read=1 << 21)
    for sweep in range(ITERS):
        even, odd, off, first, second = exchange(*out)
        mid, on = call(sides_kernel, 1, (full, rows), flags, re, im, even, odd, read=1 << 21)
        from_on = lax.ppermute(on, "row", on_chip)
        upper, to_on = call(
            on_kernel, 3, (part, rows), flags, placed, counts, mid, from_on, roots, *fixed,
            scratch=halves, flops=1 << 31, read=1 << 22,
        )
        from_on = lax.ppermute(to_on, "row", on_chip)
        total, *back = call(
            off_kernel, 3, (shape(2, 2, W, H), *sends),
            flags, placed, counts, mid, off, first, second, upper, from_on, roots, *fixed,
            scratch=halves + [pltpu.VMEM((2, 4, W, H), f32)], flops=1 << 31, read=1 << 22,
        )
        back = exchange(*back)
        more = () if sweep == ITERS - 1 else sends
        re, im, *out = call(
            step_kernel, 1, (tile, tile, *more), flags, re, im, total, *back,
            scratch=[pltpu.VMEM((2, 2, W, H), f32)], read=1 << 21,
        )
    return re, im


def solution(mesh):
    return jax.shard_map(
        shards,
        mesh=mesh,
        in_specs=(
            P("row", "col"),
            P("row", "col"),
            P(),
            P(),
            P("row", "col", None, None, None),
            P("row", "col", None, None),
            P("row", "col"),
        ),
        out_specs=(P("row", "col"), P("row", "col")),
        check_vma=False,
    )
```

```python
import math

import jax
import jax.numpy as jnp
import numpy as np
from jax import lax
from jax.experimental import pallas as pl
from jax.experimental.pallas import tpu as pltpu
from jax.sharding import PartitionSpec as P

ITERS = 2

smoothing = 0.01
step_size = 0.25

W = 256
H = 128
REACH = 80
PART = W // 2 + REACH
HALF = PART + REACH

VMEM = pl.BlockSpec(memory_space=pltpu.VMEM)
SMEM = pl.BlockSpec(memory_space=pltpu.SMEM)
f32 = jnp.float32
bf16 = jnp.bfloat16


def shape(*dims):
    return jax.ShapeDtypeStruct(dims, f32)


def dft_tables():
    k = np.arange(H)[:, None]
    mats = []
    for odd in (0, 1):
        freq = 2 * np.arange(H)[None, :] + odd
        angle = -2.0 * math.pi * ((k * freq) % W) / W
        c, s = np.cos(angle) / 16.0, np.sin(angle) / 16.0
        mats.append(np.block([[c, s], [-s, c]]))
    mats = [mats[0], mats[1], mats[0].T, mats[1].T]
    out = []
    for m in mats:
        m = m.astype(np.float32)
        hi = m.astype(jnp.bfloat16)
        lo = (m - hi.astype(np.float32)).astype(jnp.bfloat16)
        out.extend([hi, lo])
    return np.stack(out)


def split(x):
    hi = x.astype(bf16)
    lo = (x - hi.astype(f32)).astype(bf16)
    return hi, lo


def dot(a, b):
    return lax.dot_general(a, b, (((1,), (0,)), ((), ())), preferred_element_type=f32)


def right(x, tables, i):
    hi, lo = split(x)
    t_hi, t_lo = tables[2 * i], tables[2 * i + 1]
    return dot(
        jnp.concatenate([hi, lo, hi], axis=1), jnp.concatenate([t_hi, t_hi, t_lo], axis=0)
    )


def left(tables, i, x):
    hi, lo = split(x)
    t_hi, t_lo = tables[2 * i], tables[2 * i + 1]
    return dot(
        jnp.concatenate([t_hi, t_hi, t_lo], axis=1), jnp.concatenate([hi, lo, hi], axis=0)
    )


def cat(a, b, axis):
    return jnp.concatenate([a, b], axis=axis)


def roots_kernel(intensity, out):
    row = lax.broadcasted_iota(jnp.int32, (W, W), 0)
    col = lax.broadcasted_iota(jnp.int32, (W, W), 1)
    source = jnp.where(col < H, 2 * col, 2 * (col - H) + 1)
    perm = jnp.where(row == source, 1.0, 0.0).astype(bf16)
    perm3 = jnp.concatenate([perm, perm, perm], axis=0)
    for p in range(out.shape[0]):
        x = jnp.sqrt(intensity[p])
        hi = x.astype(bf16)
        rest = x - hi.astype(f32)
        mid = rest.astype(bf16)
        lo = (rest - mid.astype(f32)).astype(bf16)
        y = dot(jnp.concatenate([hi, mid, lo], axis=1), perm3)
        y = y.reshape(H, 2, W)
        out[p, pl.ds(0, H), :] = y[:, 0, :]
        out[p, pl.ds(H, H), :] = y[:, 1, :]


def rows_at(start, size):
    return pl.ds(pl.multiple_of(start, 8), size)


def columns_for(flags, left, right, even, odd):
    flip = flags[0] == 1
    for comp in range(2):
        even[comp] = jnp.where(flip, left[comp], right[comp])
        odd[comp] = jnp.where(flip, right[comp], left[comp])


def columns_from(flags, even, odd, comp):
    flip = flags[0] == 1
    return jnp.where(flip, even[comp], odd[comp]), jnp.where(flip, odd[comp], even[comp])


def pack_rows(tiles, out):
    lane = lax.broadcasted_iota(jnp.int32, (REACH, H), 1)
    gap = H - REACH
    for comp in range(2):
        for j in range(2):
            out[pl.ds((2 * comp + j) * REACH, REACH), :] = tiles(comp, 1 + j)
        out[pl.ds((4 + comp) * REACH, REACH), :] = jnp.where(lane < gap, tiles(comp, 3), tiles(comp, 0))
    rest = jnp.where(lane < REACH, tiles(0, 3), pltpu.roll(tiles(1, 3), REACH - gap, 1))
    half = REACH // 2
    inside = (lane[:half] >= gap) & (lane[:half] < gap + 64)
    out[pl.ds(6 * REACH, half), :] = jnp.where(inside, rest[:half], pltpu.roll(rest[half:], 64, 1))


def unpack_rows(packed):
    lane = lax.broadcasted_iota(jnp.int32, (REACH, H), 1)
    gap, half = H - REACH, REACH // 2
    last = packed[pl.ds(6 * REACH, half), :]
    rest = cat(last, pltpu.roll(last, 64, 1), 0)
    tiles = []
    for comp in range(2):
        outer = packed[pl.ds((4 + comp) * REACH, REACH), :]
        tail = rest if comp == 0 else pltpu.roll(rest, H - (REACH - gap), 1)
        tiles.append(
            [
                jnp.where(lane >= gap, outer, 0.0),
                packed[pl.ds(2 * comp * REACH, REACH), :],
                packed[pl.ds((2 * comp + 1) * REACH, REACH), :],
                jnp.where(lane < gap, outer, jnp.where(lane < REACH, tail, 0.0)),
            ]
        )
    return tiles


def send_columns(flags, re, im, even, odd):
    left = [x[:, 0:H].T[:REACH] for x in (re, im)]
    right = [x[:, H:W].T[H - REACH :] for x in (re, im)]
    columns_for(flags, left, right, even, odd)


def send_rows(flags, mid, on, off):
    on_rows = rows_at((W - REACH) * (1 - flags[1]), REACH)
    off_rows = rows_at((W - REACH) * flags[1], REACH)
    pack_rows(lambda comp, j: mid[comp, j, on_rows, :], on)
    pack_rows(lambda comp, j: mid[comp, j, off_rows, :], off)


def sides_kernel(flags, re, im, even, odd, mid, on, off):
    blank = jnp.zeros((H - REACH, W), f32)
    for comp, x in enumerate((re, im)):
        from_left, from_right = columns_from(flags, even, odd, comp)
        mid[comp, 0] = cat(blank, from_left, 0).T
        mid[comp, 1] = x[:, 0:H]
        mid[comp, 2] = x[:, H:W]
        mid[comp, 3] = cat(from_right, blank, 0).T
    send_rows(flags, mid, on, off)


def half_gradient(a, offsets, counts, roots, probe_re, probe_im, tables, ext, acc):
    acc[...] = jnp.zeros(acc.shape, f32)
    lane = lax.broadcasted_iota(jnp.int32, (W, H), 1)

    def position(base, carry):
        p = 2 * a + base
        shift = offsets[p, 1] - H * base
        rows = pl.ds(offsets[p, 0] - (H - REACH) - H * a, W)
        o = []
        for comp in range(2):
            rolled = [pltpu.roll(ext[comp, base + j, rows, :], H - shift, 1) for j in range(3)]
            o.append([jnp.where(lane < H - shift, rolled[j], rolled[j + 1]) for j in range(2)])
        w_re, w_im = [], []
        for j in range(2):
            p_re, p_im = probe_re[:, j * H : (j + 1) * H], probe_im[:, j * H : (j + 1) * H]
            w_re.append(o[0][j] * p_re - o[1][j] * p_im)
            w_im.append(o[0][j] * p_im + o[1][j] * p_re)
        e = right(cat(w_re[0] + w_re[1], w_im[0] + w_im[1], 1), tables, 0)
        d = right(cat(w_re[0] - w_re[1], w_im[0] - w_im[1], 1), tables, 1)
        h_re = cat(e[:, :H], d[:, :H], 1)
        h_im = cat(e[:, H:], d[:, H:], 1)
        far_e = left(tables, 2, cat(h_re[:H] + h_re[H:], h_im[:H] + h_im[H:], 0))
        far_d = left(tables, 3, cat(h_re[:H] - h_re[H:], h_im[:H] - h_im[H:], 0))

        def residual(far, root):
            power = far[:H] * far[:H] + far[H:] * far[H:] + smoothing
            factor = 1.0 - root * lax.rsqrt(power)
            return far * cat(factor, factor, 0)

        x = left(tables, 0, residual(far_e, roots[p, pl.ds(0, H), :]))
        y = left(tables, 1, residual(far_d, roots[p, pl.ds(H, H), :]))
        upper, lower = x + y, x - y
        h_re = cat(upper[:H], lower[:H], 0)
        h_im = cat(upper[H:], lower[H:], 0)
        x = right(cat(h_re[:, :H], h_im[:, :H], 1), tables, 2)
        y = right(cat(h_re[:, H:], h_im[:, H:], 1), tables, 3)
        weight = jnp.where(p < counts[0, 0], 1.0, 0.0).astype(f32)
        g_re, g_im = [], []
        for j, z in enumerate((x + y, x - y)):
            p_re, p_im = probe_re[:, j * H : (j + 1) * H], probe_im[:, j * H : (j + 1) * H]
            p_re, p_im = p_re * weight, p_im * weight
            g_re.append(z[:, :H] * p_re + z[:, H:] * p_im)
            g_im.append(z[:, H:] * p_re - z[:, :H] * p_im)
        for comp, g in enumerate((g_re, g_im)):
            r = [pltpu.roll(g[j], shift, 1) for j in range(2)]
            acc[comp, base, rows, :] += jnp.where(lane >= shift, r[0], 0.0)
            acc[comp, base + 1, rows, :] += jnp.where(lane >= shift, r[1], r[0])
            acc[comp, base + 2, rows, :] += jnp.where(lane < shift, r[1], 0.0)
        return carry

    lax.fori_loop(0, 2, position, 0)


def margin_rows(a):
    return rows_at(PART * a, REACH)


def own_rows(a):
    return rows_at(REACH - REACH * a, PART)


def covered_rows(a):
    return rows_at((W - PART) * a, PART)


def load_half(a, mid, margin, ext):
    ext[:, :, own_rows(a), :] = mid[:, :, covered_rows(a), :]
    tiles = unpack_rows(margin)
    for comp in range(2):
        for j in range(4):
            ext[comp, j, margin_rows(a), :] = tiles[comp][j]


def on_kernel(
    flags, offsets, counts, mid, on, roots, probe_re, probe_im, tables, part, to_on, ext, acc
):
    a = 1 - flags[1]
    load_half(a, mid, on, ext)
    half_gradient(a, offsets, counts, roots, probe_re, probe_im, tables, ext, acc)
    part[...] = acc[:, :, own_rows(a), :]
    pack_rows(lambda comp, j: acc[comp, j, margin_rows(a), :], to_on)


def add_rows(start, packed, out):
    tiles = unpack_rows(packed)
    for comp in range(2):
        for j in range(4):
            out[comp, j, rows_at(start, REACH), :] += tiles[comp][j]


def off_kernel(
    flags, offsets, counts, mid, off, part, on, roots, probe_re, probe_im, tables,
    centre, to_off, ext, acc,
):
    a = flags[1]
    load_half(a, mid, off, ext)
    half_gradient(a, offsets, counts, roots, probe_re, probe_im, tables, ext, acc)
    pack_rows(lambda comp, j: acc[comp, j, margin_rows(a), :], to_off)
    centre[...] = jnp.zeros(centre.shape, f32)
    centre[:, :, covered_rows(1 - a), :] = part[...]
    centre[:, :, covered_rows(a), :] += acc[:, :, own_rows(a), :]
    add_rows((W - REACH) * (1 - a), on, centre)


def rows_kernel(flags, centre, off, total, even, odd):
    total[...] = centre[...]
    add_rows((W - REACH) * flags[1], off, total)
    wide = even.shape[1] > REACH
    left, right = [], []
    for comp in range(2):
        outer = total[comp, 0].T[H - REACH :]
        left.append(cat(outer, total[comp, 1].T[:REACH], 0) if wide else outer)
        outer = total[comp, 3].T[:REACH]
        right.append(cat(total[comp, 2].T[H - REACH :], outer, 0) if wide else outer)
    columns_for(flags, left, right, even, odd)


def step_kernel(flags, mid, total, even, odd, out, to_on, to_off):
    blank = jnp.zeros((H - REACH, W), f32)
    keep_left = jnp.where(flags[2] == 1, 0.0, 1.0).astype(f32)
    keep_right = jnp.where(flags[3] == 1, 0.0, 1.0).astype(f32)
    for comp in range(2):
        from_left, from_right = columns_from(flags, even, odd, comp)
        add = [
            cat(blank, from_left[:REACH], 0).T,
            cat(from_left[REACH:], blank, 0).T,
            cat(blank, from_right[:REACH], 0).T,
            cat(from_right[REACH:], blank, 0).T,
        ]
        for j in range(4):
            value = mid[comp, j] - step_size * (total[comp, j] + add[j])
            if j in (0, 3):
                value *= keep_left if j == 0 else keep_right
            out[comp, j] = value
    send_rows(flags, out, to_on, to_off)


def final_kernel(flags, mid, total, even, odd, out_re, out_im):
    blank = jnp.zeros((H - REACH, W), f32)
    for comp, out in enumerate((out_re, out_im)):
        from_left, from_right = columns_from(flags, even, odd, comp)
        add = [cat(from_left, blank, 0).T, cat(blank, from_right, 0).T]
        for j in range(2):
            out[:, j * H : (j + 1) * H] = mid[comp, 1 + j] - step_size * (total[comp, 1 + j] + add[j])


def call(kernel, scalars, out_shape, *args, scratch=(), flops=0, read=0):
    return pl.pallas_call(
        kernel,
        in_specs=[SMEM] * scalars + [VMEM] * (len(args) - scalars),
        out_specs=jax.tree.map(lambda _: VMEM, out_shape),
        out_shape=out_shape,
        scratch_shapes=scratch,
        compiler_params=pltpu.CompilerParams(vmem_limit_bytes=48 * 1024 * 1024),
        cost_estimate=pl.CostEstimate(flops=flops, bytes_accessed=read, transcendentals=0),
    )(*args)


def swaps(size, bit):
    return [p for i in range(bit, size - 1, 2) for p in ((i, i + 1), (i + 1, i))]


def swap(x, axis, bit):
    return lax.ppermute(x, axis, swaps(lax.axis_size(axis), bit))


def columns(even, odd):
    return swap(even, "col", 0), swap(odd, "col", 1)


def shards(object_re, object_im, probe_re, probe_im, intensity, offsets, counts):
    slots = intensity.shape[2]
    placed = offsets[0, 0]
    tables = jnp.asarray(dft_tables())
    column, row = lax.axis_index("col"), lax.axis_index("row")
    last = lax.axis_size("col") - 1
    flags = jnp.stack([column % 2, row % 2, column == 0, column == last]).astype(jnp.int32)

    tile = shape(W, W)
    strip = shape(2, REACH, W)
    wide = shape(2, 2 * REACH, W)
    rows = shape(6 * REACH + REACH // 2, H)
    full = shape(2, 4, W, H)
    part = shape(2, 4, PART, H)
    halves = [pltpu.VMEM((2, 4, HALF, H), f32)] * 2
    fixed = (probe_re, probe_im, tables)

    even, odd = columns(*call(send_columns, 1, (strip, strip), flags, object_re, object_im, read=1 << 20))
    roots = call(roots_kernel, 0, shape(slots, W, W), intensity[0, 0], flops=1 << 29, read=1 << 21)
    mid, on, off = call(
        sides_kernel, 1, (full, rows, rows), flags, object_re, object_im, even, odd, read=1 << 21
    )
    for sweep in range(ITERS):
        final = sweep == ITERS - 1
        on = swap(on, "row", 0)
        off = swap(off, "row", 1)
        upper, on = call(
            on_kernel, 3, (part, rows), flags, placed, counts, mid, on, roots, *fixed,
            scratch=halves, flops=1 << 31, read=1 << 22,
        )
        on = swap(on, "row", 0)
        centre, off = call(
            off_kernel, 3, (full, rows), flags, placed, counts, mid, off, upper, on, roots, *fixed,
            scratch=halves, flops=1 << 31, read=1 << 22,
        )
        off = swap(off, "row", 1)
        strips = strip if final else wide
        total, even, odd = call(
            rows_kernel, 1, (full, strips, strips), flags, centre, off, read=1 << 21
        )
        even, odd = columns(even, odd)
        if final:
            return call(final_kernel, 1, (tile, tile), flags, mid, total, even, odd, read=1 << 21)
        mid, on, off = call(
            step_kernel, 1, (full, rows, rows), flags, mid, total, even, odd, read=1 << 21
        )


def solution(mesh):
    return jax.shard_map(
        shards,
        mesh=mesh,
        in_specs=(
            P("row", "col"),
            P("row", "col"),
            P(),
            P(),
            P("row", "col", None, None, None),
            P("row", "col", None, None),
            P("row", "col"),
        ),
        out_specs=(P("row", "col"), P("row", "col")),
        check_vma=False,
    )
```

```python
import math

import jax
import jax.numpy as jnp
import numpy as np
from jax import lax
from jax.experimental import pallas as pl
from jax.experimental.pallas import tpu as pltpu
from jax.sharding import PartitionSpec as P

ITERS = 2

smoothing = 0.01
step_size = 0.25

W = 256
H = 128
REACH = 80
PART = W // 2 + REACH
HALF = PART + REACH

VMEM = pl.BlockSpec(memory_space=pltpu.VMEM)
SMEM = pl.BlockSpec(memory_space=pltpu.SMEM)
ANY = pl.BlockSpec(memory_space=pltpu.HBM)
f32 = jnp.float32
bf16 = jnp.bfloat16


def shape(*dims):
    return jax.ShapeDtypeStruct(dims, f32)


def dft_tables():
    k = np.arange(H)[:, None]
    mats = []
    for odd in (0, 1):
        freq = 2 * np.arange(H)[None, :] + odd
        angle = -2.0 * math.pi * ((k * freq) % W) / W
        c, s = np.cos(angle) / 16.0, np.sin(angle) / 16.0
        mats.append(np.block([[c, s], [-s, c]]))
    mats = [mats[0], mats[1], mats[0].T, mats[1].T]
    out = []
    for m in mats:
        m = m.astype(np.float32)
        hi = m.astype(jnp.bfloat16)
        lo = (m - hi.astype(np.float32)).astype(jnp.bfloat16)
        out.extend([hi, lo])
    return np.stack(out)


def split(x):
    hi = x.astype(bf16)
    lo = (x - hi.astype(f32)).astype(bf16)
    return hi, lo


def dot(a, b):
    return lax.dot_general(a, b, (((1,), (0,)), ((), ())), preferred_element_type=f32)


def right(x, tables, i):
    hi, lo = split(x)
    t_hi, t_lo = tables[2 * i], tables[2 * i + 1]
    return dot(
        jnp.concatenate([hi, lo, hi], axis=1), jnp.concatenate([t_hi, t_hi, t_lo], axis=0)
    )


def left(tables, i, x):
    hi, lo = split(x)
    t_hi, t_lo = tables[2 * i], tables[2 * i + 1]
    return dot(
        jnp.concatenate([t_hi, t_hi, t_lo], axis=1), jnp.concatenate([hi, lo, hi], axis=0)
    )


def cat(a, b, axis):
    return jnp.concatenate([a, b], axis=axis)


def roots_kernel(
    flags, intensity, probe_re, probe_im, tables, out, probe_out, tables_out, held, sems
):
    slots = out.shape[0]
    copies = [pltpu.make_async_copy(intensity.at[p], held.at[p], sems.at[p]) for p in range(slots)]
    for comp, x in enumerate((probe_re, probe_im)):
        for j in range(2):
            k = 2 * comp + j
            copies.append(
                pltpu.make_async_copy(
                    x.at[:, pl.ds(j * H, H)], probe_out.at[comp, j], sems.at[slots + k]
                )
            )
    copies.append(pltpu.make_async_copy(tables, tables_out, sems.at[slots + 4]))
    for c in copies:
        c.start()
    row = lax.broadcasted_iota(jnp.int32, (W, W), 0)
    col = lax.broadcasted_iota(jnp.int32, (W, W), 1)
    source = jnp.where(col < H, 2 * col, 2 * (col - H) + 1)
    perm = jnp.where(row == source, 1.0, 0.0).astype(bf16)
    perm3 = jnp.concatenate([perm, perm, perm], axis=0)
    for p in range(slots):
        copies[p].wait()
        x = jnp.sqrt(held[p])
        hi = x.astype(bf16)
        rest = x - hi.astype(f32)
        mid = rest.astype(bf16)
        lo = (rest - mid.astype(f32)).astype(bf16)
        y = dot(jnp.concatenate([hi, mid, lo], axis=1), perm3)
        y = y.reshape(H, 2, W)
        out[p, pl.ds(0, H), :] = y[:, 0, :]
        out[p, pl.ds(H, H), :] = y[:, 1, :]
    for c in copies[slots:]:
        c.wait()


OFFSETS = 5
COUNT = 13


def rows_at(start, size):
    return pl.ds(pl.multiple_of(start, 8), size)


def columns_for(flags, left, right, even, odd):
    flip = flags[0] == 1
    for comp in range(2):
        even[comp] = jnp.where(flip, left[comp], right[comp])
        odd[comp] = jnp.where(flip, right[comp], left[comp])


def columns_from(flags, even, odd, comp):
    flip = flags[0] == 1
    e = even[comp]
    o = jnp.where(flags[2] + flags[3] == 0, odd[comp], 0.0)
    return jnp.where(flip, e, o), jnp.where(flip, o, e)


def pack_rows(tiles, out):
    lane = lax.broadcasted_iota(jnp.int32, (REACH, H), 1)
    gap = H - REACH
    for comp in range(2):
        for j in range(2):
            out[pl.ds((2 * comp + j) * REACH, REACH), :] = tiles(comp, 1 + j)
        out[pl.ds((4 + comp) * REACH, REACH), :] = jnp.where(lane < gap, tiles(comp, 3), tiles(comp, 0))
    rest = jnp.where(lane < REACH, tiles(0, 3), pltpu.roll(tiles(1, 3), REACH - gap, 1))
    half = REACH // 2
    inside = (lane[:half] >= gap) & (lane[:half] < gap + 64)
    out[pl.ds(6 * REACH, half), :] = jnp.where(inside, rest[:half], pltpu.roll(rest[half:], 64, 1))


def unpack_rows(packed, keep=None):
    def load(start, size):
        x = packed[pl.ds(start, size), :]
        return x if keep is None else jnp.where(keep, x, 0.0)

    lane = lax.broadcasted_iota(jnp.int32, (REACH, H), 1)
    gap, half = H - REACH, REACH // 2
    last = load(6 * REACH, half)
    rest = cat(last, pltpu.roll(last, 64, 1), 0)
    tiles = []
    for comp in range(2):
        outer = load((4 + comp) * REACH, REACH)
        tail = rest if comp == 0 else pltpu.roll(rest, H - (REACH - gap), 1)
        tiles.append(
            [
                jnp.where(lane >= gap, outer, 0.0),
                load(2 * comp * REACH, REACH),
                load((2 * comp + 1) * REACH, REACH),
                jnp.where(lane < gap, outer, jnp.where(lane < REACH, tail, 0.0)),
            ]
        )
    return tiles


def send_columns(flags, mid, even, odd):
    left = [mid[comp, 1].T[:REACH] for comp in range(2)]
    right = [mid[comp, 2].T[H - REACH :] for comp in range(2)]
    columns_for(flags, left, right, even, odd)


def send_rows(flags, mid, on, off):
    on_rows = rows_at((W - REACH) * (1 - flags[1]), REACH)
    off_rows = rows_at((W - REACH) * flags[1], REACH)
    pack_rows(lambda comp, j: mid[comp, j, on_rows, :], on)
    pack_rows(lambda comp, j: mid[comp, j, off_rows, :], off)


def sides_kernel(flags, even, odd, mid, out, on, off):
    blank = jnp.zeros((H - REACH, W), f32)
    for comp in range(2):
        from_left, from_right = columns_from(flags, even, odd, comp)
        out[comp, 0] = cat(blank, from_left, 0).T
        out[comp, 3] = cat(from_right, blank, 0).T
    send_rows(flags, out, on, off)


def half_gradient(a, flags, roots, probe, tables, ext, acc):
    acc[...] = jnp.zeros(acc.shape, f32)
    lane = lax.broadcasted_iota(jnp.int32, (W, H), 1)

    def position(base, carry):
        p = 2 * a + base
        shift = flags[OFFSETS + 2 * p + 1] - H * base
        rows = pl.ds(flags[OFFSETS + 2 * p] - (H - REACH) - H * a, W)
        o = []
        for comp in range(2):
            rolled = [pltpu.roll(ext[comp, base + j, rows, :], H - shift, 1) for j in range(3)]
            o.append([jnp.where(lane < H - shift, rolled[j], rolled[j + 1]) for j in range(2)])
        w_re, w_im = [], []
        for j in range(2):
            p_re, p_im = probe[0, j], probe[1, j]
            w_re.append(o[0][j] * p_re - o[1][j] * p_im)
            w_im.append(o[0][j] * p_im + o[1][j] * p_re)
        e = right(cat(w_re[0] + w_re[1], w_im[0] + w_im[1], 1), tables, 0)
        d = right(cat(w_re[0] - w_re[1], w_im[0] - w_im[1], 1), tables, 1)
        h_re = cat(e[:, :H], d[:, :H], 1)
        h_im = cat(e[:, H:], d[:, H:], 1)
        far_e = left(tables, 2, cat(h_re[:H] + h_re[H:], h_im[:H] + h_im[H:], 0))
        far_d = left(tables, 3, cat(h_re[:H] - h_re[H:], h_im[:H] - h_im[H:], 0))

        def residual(far, root):
            power = far[:H] * far[:H] + far[H:] * far[H:] + smoothing
            factor = 1.0 - root * lax.rsqrt(power)
            return far * cat(factor, factor, 0)

        x = left(tables, 0, residual(far_e, roots[p, pl.ds(0, H), :]))
        y = left(tables, 1, residual(far_d, roots[p, pl.ds(H, H), :]))
        upper, lower = x + y, x - y
        h_re = cat(upper[:H], lower[:H], 0)
        h_im = cat(upper[H:], lower[H:], 0)
        x = right(cat(h_re[:, :H], h_im[:, :H], 1), tables, 2)
        y = right(cat(h_re[:, H:], h_im[:, H:], 1), tables, 3)
        weight = jnp.where(p < flags[COUNT], 1.0, 0.0).astype(f32)
        g_re, g_im = [], []
        for j, z in enumerate((x + y, x - y)):
            p_re, p_im = probe[0, j] * weight, probe[1, j] * weight
            g_re.append(z[:, :H] * p_re + z[:, H:] * p_im)
            g_im.append(z[:, H:] * p_re - z[:, :H] * p_im)
        for comp, g in enumerate((g_re, g_im)):
            r = [pltpu.roll(g[j], shift, 1) for j in range(2)]
            acc[comp, base, rows, :] += jnp.where(lane >= shift, r[0], 0.0)
            acc[comp, base + 1, rows, :] += jnp.where(lane >= shift, r[1], r[0])
            acc[comp, base + 2, rows, :] += jnp.where(lane < shift, r[1], 0.0)
        return carry

    lax.fori_loop(0, 2, position, 0)


def margin_rows(a):
    return rows_at(PART * a, REACH)


def own_rows(a):
    return rows_at(REACH - REACH * a, PART)


def covered_rows(a):
    return rows_at((W - PART) * a, PART)


def load_half(a, mid, margin, ext, keep=None):
    ext[:, :, own_rows(a), :] = mid[:, :, covered_rows(a), :]
    tiles = unpack_rows(margin, keep)
    for comp in range(2):
        for j in range(4):
            ext[comp, j, margin_rows(a), :] = tiles[comp][j]


def on_kernel(flags, mid, on, roots, probe, tables, part, to_on, ext, acc):
    a = 1 - flags[1]
    load_half(a, mid, on, ext)
    half_gradient(a, flags, roots, probe, tables, ext, acc)
    part[...] = acc[:, :, own_rows(a), :]
    pack_rows(lambda comp, j: acc[comp, j, margin_rows(a), :], to_on)


def add_rows(start, packed, out, keep=None):
    tiles = unpack_rows(packed, keep)
    for comp in range(2):
        for j in range(4):
            out[comp, j, rows_at(start, REACH), :] += tiles[comp][j]


def off_kernel(flags, mid, off, part, on, roots, probe, tables, centre, to_off, ext, acc):
    a = flags[1]
    load_half(a, mid, off, ext, flags[4] == 0)
    half_gradient(a, flags, roots, probe, tables, ext, acc)
    pack_rows(lambda comp, j: acc[comp, j, margin_rows(a), :], to_off)
    centre[...] = jnp.zeros(centre.shape, f32)
    centre[:, :, covered_rows(1 - a), :] = part[...]
    centre[:, :, covered_rows(a), :] += acc[:, :, own_rows(a), :]
    add_rows((W - REACH) * (1 - a), on, centre)


def rows_kernel(flags, centre, off, total, even, odd):
    add_rows((W - REACH) * flags[1], off, total, flags[4] == 0)
    wide = even.shape[1] > REACH
    left, right = [], []
    for comp in range(2):
        outer = total[comp, 0].T[H - REACH :]
        left.append(cat(outer, total[comp, 1].T[:REACH], 0) if wide else outer)
        outer = total[comp, 3].T[:REACH]
        right.append(cat(total[comp, 2].T[H - REACH :], outer, 0) if wide else outer)
    columns_for(flags, left, right, even, odd)


def step_kernel(flags, mid, total, even, odd, out, to_on, to_off):
    blank = jnp.zeros((H - REACH, W), f32)
    keep_left = jnp.where(flags[2] == 1, 0.0, 1.0).astype(f32)
    keep_right = jnp.where(flags[3] == 1, 0.0, 1.0).astype(f32)
    for comp in range(2):
        from_left, from_right = columns_from(flags, even, odd, comp)
        add = [
            cat(blank, from_left[:REACH], 0).T,
            cat(from_left[REACH:], blank, 0).T,
            cat(blank, from_right[:REACH], 0).T,
            cat(from_right[REACH:], blank, 0).T,
        ]
        for j in range(4):
            value = mid[comp, j] - step_size * (total[comp, j] + add[j])
            if j in (0, 3):
                value *= keep_left if j == 0 else keep_right
            out[comp, j] = value
    send_rows(flags, out, to_on, to_off)


def final_kernel(flags, mid, total, even, odd, out_re, out_im):
    blank = jnp.zeros((H - REACH, W), f32)
    for comp, out in enumerate((out_re, out_im)):
        from_left, from_right = columns_from(flags, even, odd, comp)
        add = [cat(from_left, blank, 0).T, cat(blank, from_right, 0).T]
        for j in range(2):
            out[:, j * H : (j + 1) * H] = mid[comp, 1 + j] - step_size * (total[comp, 1 + j] + add[j])


def call(kernel, specs, out_shape, *args, scratch=(), flops=0, read=0, alias={}):
    return pl.pallas_call(
        kernel,
        in_specs=[SMEM] + specs + [VMEM] * (len(args) - 1 - len(specs)),
        out_specs=jax.tree.map(lambda _: VMEM, out_shape),
        out_shape=out_shape,
        scratch_shapes=scratch,
        input_output_aliases=alias,
        compiler_params=pltpu.CompilerParams(vmem_limit_bytes=24 * 1024 * 1024),
        cost_estimate=pl.CostEstimate(flops=flops, bytes_accessed=read, transcendentals=0),
    )(*args)


def swaps(size, bit):
    return [p for i in range(bit, size, 2) for p in ((i, (i + 1) % size), ((i + 1) % size, i))]


def swap(x, axis, bit):
    return lax.ppermute(x, axis, swaps(lax.axis_size(axis), bit))


def columns(even, odd):
    return swap(even, "col", 0), swap(odd, "col", 1)


def shards(object_re, object_im, probe_re, probe_im, intensity, offsets, counts):
    slots = intensity.shape[2]
    column, row = lax.axis_index("col"), lax.axis_index("row")
    last, lowest = lax.axis_size("col") - 1, lax.axis_size("row") - 1
    edge = (row == 0) | (row == lowest)
    flags = jnp.stack([column % 2, row % 2, column == 0, column == last, edge]).astype(jnp.int32)
    known = jnp.concatenate([flags, offsets.reshape(-1), counts.reshape(-1)])

    tile = shape(W, W)
    strip = shape(2, REACH, W)
    wide = shape(2, 2 * REACH, W)
    rows = shape(6 * REACH + REACH // 2, H)
    full = shape(2, 4, W, H)
    part = shape(2, 4, PART, H)
    halves = [pltpu.VMEM((2, 4, HALF, H), f32)] * 2

    blank = jnp.zeros((W, H), f32)
    mid = jnp.stack(
        [jnp.stack([blank, x[:, 0:H], x[:, H:W], blank]) for x in (object_re, object_im)]
    )
    even, odd = call(send_columns, [], (strip, strip), flags, mid, read=1 << 20)
    even, odd = columns(even, odd)
    tables = jnp.asarray(dft_tables())
    fixed = call(
        roots_kernel,
        [ANY] * 4,
        (shape(slots, W, W), shape(2, 2, W, H), jax.ShapeDtypeStruct(tables.shape, bf16)),
        known, intensity[0, 0], probe_re, probe_im, tables,
        scratch=[pltpu.VMEM((slots, W, W), f32), pltpu.SemaphoreType.DMA((slots + 5,))],
        flops=1 << 29, read=1 << 21,
    )
    mid, on, off = call(
        sides_kernel, [], (full, rows, rows), flags, even, odd, mid, read=1 << 21, alias={3: 0}
    )
    for sweep in range(ITERS):
        final = sweep == ITERS - 1
        on = swap(on, "row", 0)
        off = swap(off, "row", 1)
        upper, on = call(
            on_kernel, [], (part, rows), known, mid, on, *fixed,
            scratch=halves, flops=1 << 31, read=1 << 22,
        )
        on = swap(on, "row", 0)
        centre, off = call(
            off_kernel, [], (full, rows), known, mid, off, upper, on, *fixed,
            scratch=halves, flops=1 << 31, read=1 << 22,
        )
        off = swap(off, "row", 1)
        strips = strip if final else wide
        total, even, odd = call(
            rows_kernel, [], (full, strips, strips), known, centre, off, read=1 << 21, alias={1: 0}
        )
        even, odd = columns(even, odd)
        if final:
            return call(final_kernel, [], (tile, tile), known, mid, total, even, odd, read=1 << 21)
        mid, on, off = call(
            step_kernel, [], (full, rows, rows), known, mid, total, even, odd, read=1 << 21,
            alias={1: 0},
        )


def solution(mesh):
    return jax.shard_map(
        shards,
        mesh=mesh,
        in_specs=(
            P("row", "col"),
            P("row", "col"),
            P(),
            P(),
            P("row", "col", None, None, None),
            P("row", "col", None, None),
            P("row", "col"),
        ),
        out_specs=(P("row", "col"), P("row", "col")),
        check_vma=False,
    )
```

```python
import functools
import math

import jax
import jax.numpy as jnp
import numpy as np
from jax import lax
from jax.experimental import pallas as pl
from jax.experimental.pallas import tpu as pltpu
from jax.sharding import PartitionSpec as P

ITERS = 2

smoothing = 0.01
step_size = 0.25

W = 256
H = 128
REACH = 80
PART = W // 2 + REACH
HALF = PART + REACH

VMEM = pl.BlockSpec(memory_space=pltpu.VMEM)
SMEM = pl.BlockSpec(memory_space=pltpu.SMEM)
ANY = pl.BlockSpec(memory_space=pltpu.HBM)
f32 = jnp.float32
bf16 = jnp.bfloat16


def shape(*dims):
    return jax.ShapeDtypeStruct(dims, f32)


def dft_tables():
    k = np.arange(H)[:, None]
    mats = []
    for odd in (0, 1):
        freq = 2 * np.arange(H)[None, :] + odd
        angle = -2.0 * math.pi * ((k * freq) % W) / W
        c, s = np.cos(angle) / 16.0, np.sin(angle) / 16.0
        mats.append(np.block([[c, s], [-s, c]]))
    mats = [mats[0], mats[1], mats[0].T, mats[1].T]
    out = []
    for m in mats:
        m = m.astype(np.float32)
        hi = m.astype(jnp.bfloat16)
        lo = (m - hi.astype(np.float32)).astype(jnp.bfloat16)
        out.extend([hi, lo])
    return np.stack(out)


def split(x):
    hi = x.astype(bf16)
    lo = (x - hi.astype(f32)).astype(bf16)
    return hi, lo


def dot(a, b):
    return lax.dot_general(a, b, (((1,), (0,)), ((), ())), preferred_element_type=f32)


def right(x, tables, i):
    hi, lo = split(x)
    t_hi, t_lo = tables[2 * i], tables[2 * i + 1]
    return dot(
        jnp.concatenate([hi, lo, hi], axis=1), jnp.concatenate([t_hi, t_hi, t_lo], axis=0)
    )


def left(tables, i, x):
    hi, lo = split(x)
    t_hi, t_lo = tables[2 * i], tables[2 * i + 1]
    return dot(
        jnp.concatenate([t_hi, t_hi, t_lo], axis=1), jnp.concatenate([hi, lo, hi], axis=0)
    )


def cat(a, b, axis):
    return jnp.concatenate([a, b], axis=axis)


def roots_kernel(
    flags, intensity, probe_re, probe_im, tables, out, probe_out, tables_out, held, sems
):
    slots = out.shape[0]
    copies = [pltpu.make_async_copy(intensity.at[p], held.at[p], sems.at[p]) for p in range(slots)]
    for comp, x in enumerate((probe_re, probe_im)):
        for j in range(2):
            k = 2 * comp + j
            copies.append(
                pltpu.make_async_copy(
                    x.at[:, pl.ds(j * H, H)], probe_out.at[comp, j], sems.at[slots + k]
                )
            )
    copies.append(pltpu.make_async_copy(tables, tables_out, sems.at[slots + 4]))
    for c in copies:
        c.start()
    row = lax.broadcasted_iota(jnp.int32, (W, W), 0)
    col = lax.broadcasted_iota(jnp.int32, (W, W), 1)
    source = jnp.where(col < H, 2 * col, 2 * (col - H) + 1)
    perm = jnp.where(row == source, 1.0, 0.0).astype(bf16)
    perm3 = jnp.concatenate([perm, perm, perm], axis=0)
    for p in range(slots):
        copies[p].wait()
        x = jnp.sqrt(held[p])
        hi = x.astype(bf16)
        rest = x - hi.astype(f32)
        mid = rest.astype(bf16)
        lo = (rest - mid.astype(f32)).astype(bf16)
        y = dot(jnp.concatenate([hi, mid, lo], axis=1), perm3)
        y = y.reshape(H, 2, W)
        out[p, pl.ds(0, H), :] = y[:, 0, :]
        out[p, pl.ds(H, H), :] = y[:, 1, :]
    for c in copies[slots:]:
        c.wait()


OFFSETS = 5
COUNT = 13
GAP = H - REACH
SIDE = 3 * REACH + 24


def rows_at(start, size):
    return pl.ds(pl.multiple_of(start, 8), size)


def side(flags, odd):
    left = 1 - flags[0] if odd else flags[0]
    return left, 2 - left, 3 - 3 * left


def inside(flags, odd):
    return flags[2] + flags[3] == 0 if odd else None


def masked(keep, x):
    return x if keep is None else jnp.where(keep, x, 0.0)


def own_columns(left, x):
    return jnp.where(left == 1, x[:REACH], x[GAP:])


def margin_columns(left, x):
    return jnp.where(left == 1, x[GAP:], x[:REACH])


def columns_out(flags, odd, tiles, out):
    left, inner, outer = side(flags, odd)
    for comp in range(2):
        if out.shape[1] == REACH:
            out[comp] = margin_columns(left, tiles[comp, outer].T)
        else:
            out[comp, 0:REACH] = own_columns(left, tiles[comp, inner].T)
            out[comp, REACH:] = margin_columns(left, tiles[comp, outer].T)


def columns_at(low, x):
    blank = jnp.zeros((GAP, W), f32)
    return jnp.where(low, cat(x, blank, 0), cat(blank, x, 0)).T


def pack_side(flags, odd, tiles, rows, out):
    left, inner, outer = side(flags, odd)
    lane = lax.broadcasted_iota(jnp.int32, (REACH, H), 1)
    for comp in range(2):
        out[pl.ds(comp * REACH, REACH), :] = tiles[comp, inner, rows, :]
    re, im = (pltpu.roll(tiles[comp, outer, rows, :], REACH * left, 1) for comp in range(2))
    out[pl.ds(2 * REACH, REACH), :] = jnp.where(lane < REACH, re, pltpu.roll(im, REACH, 1))
    rest = jnp.zeros((24, H), f32)
    for g in range(4):
        part = im[24 * g : min(24 * g + 24, REACH)]
        part = pltpu.roll(part, (32 * g - GAP) % H, 1)
        if part.shape[0] < 24:
            part = cat(part, jnp.zeros((24 - part.shape[0], H), f32), 0)
        rest = jnp.where(lane[:24] // 32 == g, part, rest)
    out[pl.ds(3 * REACH, 24), :] = rest


def unpack_side(flags, odd, packed, keep):
    left, _, _ = side(flags, odd)
    lane = lax.broadcasted_iota(jnp.int32, (REACH, H), 1)
    mixed = masked(keep, packed[pl.ds(2 * REACH, REACH), :])
    rest = masked(keep, packed[pl.ds(3 * REACH, 24), :])
    tail = jnp.concatenate(
        [pltpu.roll(rest, (GAP - 32 * g) % H, 1)[: min(24, REACH - 24 * g)] for g in range(4)], axis=0
    )
    re = jnp.where(lane < REACH, mixed, 0.0)
    im = jnp.where(lane < GAP, pltpu.roll(mixed, GAP, 1), jnp.where(lane < REACH, tail, 0.0))
    return [
        (masked(keep, packed[pl.ds(comp * REACH, REACH), :]), pltpu.roll(x, GAP * left, 1))
        for comp, x in enumerate((re, im))
    ]


def put_side(flags, odd, packed, tiles, rows, add):
    _, inner, outer = side(flags, odd)
    for comp, pair in enumerate(unpack_side(flags, odd, packed, flags[4] == 0)):
        for tile, x in zip((inner, outer), pair):
            if add:
                tiles[comp, tile, rows, :] += x
            else:
                tiles[comp, tile, rows, :] = x


def first_kernel(flags, mid, even, odd):
    for is_odd, out in enumerate((even, odd)):
        left, inner, _ = side(flags, is_odd)
        for comp in range(2):
            out[comp] = own_columns(left, mid[comp, inner].T)


def send_rows(flags, odd, tiles, off, on):
    pack_side(flags, odd, tiles, rows_at((W - REACH) * flags[1], REACH), off)
    for ref in on:
        ref[...] = tiles[:, :, rows_at((W - REACH) * (1 - flags[1]), REACH), :]


def margin_kernel(odd, flags, strip, mid, out, off, *on):
    left, _, outer = side(flags, odd)
    for comp in range(2):
        out[comp, outer] = columns_at(left == 0, masked(inside(flags, odd), strip[comp]))
    send_rows(flags, odd, out, off, on)


def half_gradient(a, flags, roots, probe, tables, ext, acc):
    acc[...] = jnp.zeros(acc.shape, f32)
    lane = lax.broadcasted_iota(jnp.int32, (W, H), 1)

    def position(base, carry):
        p = 2 * a + base
        shift = flags[OFFSETS + 2 * p + 1] - H * base
        rows = pl.ds(flags[OFFSETS + 2 * p] - (H - REACH) - H * a, W)
        o = []
        for comp in range(2):
            rolled = [pltpu.roll(ext[comp, base + j, rows, :], H - shift, 1) for j in range(3)]
            o.append([jnp.where(lane < H - shift, rolled[j], rolled[j + 1]) for j in range(2)])
        w_re, w_im = [], []
        for j in range(2):
            p_re, p_im = probe[0, j], probe[1, j]
            w_re.append(o[0][j] * p_re - o[1][j] * p_im)
            w_im.append(o[0][j] * p_im + o[1][j] * p_re)
        e = right(cat(w_re[0] + w_re[1], w_im[0] + w_im[1], 1), tables, 0)
        d = right(cat(w_re[0] - w_re[1], w_im[0] - w_im[1], 1), tables, 1)
        h_re = cat(e[:, :H], d[:, :H], 1)
        h_im = cat(e[:, H:], d[:, H:], 1)
        far_e = left(tables, 2, cat(h_re[:H] + h_re[H:], h_im[:H] + h_im[H:], 0))
        far_d = left(tables, 3, cat(h_re[:H] - h_re[H:], h_im[:H] - h_im[H:], 0))

        def residual(far, root):
            power = far[:H] * far[:H] + far[H:] * far[H:] + smoothing
            factor = 1.0 - root * lax.rsqrt(power)
            return far * cat(factor, factor, 0)

        x = left(tables, 0, residual(far_e, roots[p, pl.ds(0, H), :]))
        y = left(tables, 1, residual(far_d, roots[p, pl.ds(H, H), :]))
        upper, lower = x + y, x - y
        h_re = cat(upper[:H], lower[:H], 0)
        h_im = cat(upper[H:], lower[H:], 0)
        x = right(cat(h_re[:, :H], h_im[:, :H], 1), tables, 2)
        y = right(cat(h_re[:, H:], h_im[:, H:], 1), tables, 3)
        weight = jnp.where(p < flags[COUNT], 1.0, 0.0).astype(f32)
        g_re, g_im = [], []
        for j, z in enumerate((x + y, x - y)):
            p_re, p_im = probe[0, j] * weight, probe[1, j] * weight
            g_re.append(z[:, :H] * p_re + z[:, H:] * p_im)
            g_im.append(z[:, H:] * p_re - z[:, :H] * p_im)
        for comp, g in enumerate((g_re, g_im)):
            r = [pltpu.roll(g[j], shift, 1) for j in range(2)]
            acc[comp, base, rows, :] += jnp.where(lane >= shift, r[0], 0.0)
            acc[comp, base + 1, rows, :] += jnp.where(lane >= shift, r[1], r[0])
            acc[comp, base + 2, rows, :] += jnp.where(lane < shift, r[1], 0.0)
        return carry

    lax.fori_loop(0, 2, position, 0)


def margin_rows(a):
    return rows_at(PART * a, REACH)


def own_rows(a):
    return rows_at(REACH - REACH * a, PART)


def covered_rows(a):
    return rows_at((W - PART) * a, PART)


def load_half(a, mid, ext):
    ext[:, :, own_rows(a), :] = mid[:, :, covered_rows(a), :]


def on_kernel(flags, mid, on, roots, probe, tables, part, to_on, ext, acc):
    a = 1 - flags[1]
    load_half(a, mid, ext)
    ext[:, :, margin_rows(a), :] = on[...]
    half_gradient(a, flags, roots, probe, tables, ext, acc)
    part[...] = acc[:, :, own_rows(a), :]
    to_on[...] = acc[:, :, margin_rows(a), :]


def off_kernel(flags, mid, even, odd, part, on, roots, probe, tables, centre, to_even, to_odd, ext, acc):
    a = flags[1]
    load_half(a, mid, ext)
    put_side(flags, 0, even, ext, margin_rows(a), False)
    put_side(flags, 1, odd, ext, margin_rows(a), False)
    half_gradient(a, flags, roots, probe, tables, ext, acc)
    pack_side(flags, 0, acc, margin_rows(a), to_even)
    pack_side(flags, 1, acc, margin_rows(a), to_odd)
    centre[...] = jnp.zeros(centre.shape, f32)
    centre[:, :, covered_rows(1 - a), :] = part[...]
    centre[:, :, covered_rows(a), :] += acc[:, :, own_rows(a), :]
    centre[:, :, rows_at((W - REACH) * (1 - a), REACH), :] += on[...]


def rows_kernel(odd, flags, centre, off, total, strip):
    put_side(flags, odd, off, total, rows_at((W - REACH) * flags[1], REACH), True)
    columns_out(flags, odd, total, strip)


def step_kernel(odd, flags, mid, total, strip, out, off, *on):
    left, inner, outer = side(flags, odd)
    keep = inside(flags, odd)
    for comp in range(2):
        got = masked(keep, strip[comp])
        x = total[comp, outer] + columns_at(left == 0, got[:REACH])
        out[comp, outer] = masked(keep, mid[comp, outer] - step_size * x)
        x = total[comp, inner] + columns_at(left == 1, got[REACH:])
        out[comp, inner] = mid[comp, inner] - step_size * x
    send_rows(flags, odd, out, off, on)


def final_kernel(flags, mid, total, even, odd, out_re, out_im):
    for comp, out in enumerate((out_re, out_im)):
        for is_odd, strip in enumerate((even, odd)):
            left, inner, _ = side(flags, is_odd)
            got = columns_at(left == 1, masked(inside(flags, is_odd), strip[comp]))
            value = mid[comp, inner] - step_size * (total[comp, inner] + got)
            out[:, pl.ds(pl.multiple_of(H * (inner - 1), H), H)] = value


def call(kernel, specs, out_shape, *args, scratch=(), flops=0, read=0, alias={}):
    return pl.pallas_call(
        kernel,
        in_specs=[SMEM] + specs + [VMEM] * (len(args) - 1 - len(specs)),
        out_specs=jax.tree.map(lambda _: VMEM, out_shape),
        out_shape=out_shape,
        scratch_shapes=scratch,
        input_output_aliases=alias,
        compiler_params=pltpu.CompilerParams(vmem_limit_bytes=24 * 1024 * 1024),
        cost_estimate=pl.CostEstimate(flops=flops, bytes_accessed=read, transcendentals=0),
    )(*args)


def swaps(size, bit):
    return [p for i in range(bit, size, 2) for p in ((i, (i + 1) % size), ((i + 1) % size, i))]


def swap(x, axis, bit):
    return lax.ppermute(x, axis, swaps(lax.axis_size(axis), bit))


def shards(object_re, object_im, probe_re, probe_im, intensity, offsets, counts):
    slots = intensity.shape[2]
    column, row = lax.axis_index("col"), lax.axis_index("row")
    last, lowest = lax.axis_size("col") - 1, lax.axis_size("row") - 1
    edge = (row == 0) | (row == lowest)
    flags = jnp.stack([column % 2, row % 2, column == 0, column == last, edge]).astype(jnp.int32)
    known = jnp.concatenate([flags, offsets.reshape(-1), counts.reshape(-1)])

    tile = shape(W, W)
    narrow = shape(2, REACH, W)
    wide = shape(2, 2 * REACH, W)
    half = shape(SIDE, H)
    rows = shape(2, 4, REACH, H)
    full = shape(2, 4, W, H)
    part = shape(2, 4, PART, H)
    halves = [pltpu.VMEM((2, 4, HALF, H), f32)] * 2

    def named(kernel, *args, **options):
        return call(kernel, [], *args, **options)

    for sweep in range(ITERS + 1):
        if sweep == 0:
            blank = jnp.zeros((W, H), f32)
            mid = jnp.stack(
                [jnp.stack([blank, x[:, 0:H], x[:, H:W], blank]) for x in (object_re, object_im)]
            )
            even, odd = named(first_kernel, (narrow, narrow), flags, mid, read=1 << 20)
            even, odd = swap(even, "col", 0), swap(odd, "col", 1)
            tables = jnp.asarray(dft_tables())
            fixed = call(
                roots_kernel,
                [ANY] * 4,
                (shape(slots, W, W), shape(2, 2, W, H), jax.ShapeDtypeStruct(tables.shape, bf16)),
                known, intensity[0, 0], probe_re, probe_im, tables,
                scratch=[pltpu.VMEM((slots, W, W), f32), pltpu.SemaphoreType.DMA((slots + 5,))],
                flops=1 << 29, read=1 << 21,
            )
        else:
            strip = narrow if sweep == ITERS else wide
            to_even = swap(to_even, "row", 1)
            to_odd = swap(to_odd, "row", 1)
            total, even = named(
                functools.partial(rows_kernel, 0), (full, strip), known, total, to_even,
                read=1 << 20, alias={1: 0},
            )
            even = swap(even, "col", 0)
            total, odd = named(
                functools.partial(rows_kernel, 1), (full, strip), known, total, to_odd,
                read=1 << 20, alias={1: 0},
            )
            odd = swap(odd, "col", 1)
        if sweep == ITERS:
            return named(final_kernel, (tile, tile), known, mid, total, even, odd, read=1 << 21)
        if sweep == 0:
            mid, to_even = named(
                functools.partial(margin_kernel, 0), (full, half), known, even, mid,
                read=1 << 20, alias={2: 0},
            )
            to_even = swap(to_even, "row", 1)
            mid, to_odd, on = named(
                functools.partial(margin_kernel, 1), (full, half, rows), known, odd, mid,
                read=1 << 20, alias={2: 0},
            )
        else:
            mid, to_even = named(
                functools.partial(step_kernel, 0), (full, half), known, mid, total, even,
                read=1 << 20, alias={1: 0},
            )
            to_even = swap(to_even, "row", 1)
            mid, to_odd, on = named(
                functools.partial(step_kernel, 1), (full, half, rows), known, mid, total, odd,
                read=1 << 20, alias={1: 0},
            )
        on = swap(on, "row", 0)
        to_odd = swap(to_odd, "row", 1)
        upper, on = named(
            on_kernel, (part, rows), known, mid, on, *fixed,
            scratch=halves, flops=1 << 31, read=1 << 22,
        )
        on = swap(on, "row", 0)
        total, to_even, to_odd = named(
            off_kernel, (full, half, half), known, mid, to_even, to_odd, upper, on, *fixed,
            scratch=halves, flops=1 << 31, read=1 << 22,
        )


def solution(mesh):
    return jax.shard_map(
        shards,
        mesh=mesh,
        in_specs=(
            P("row", "col"),
            P("row", "col"),
            P(),
            P(),
            P("row", "col", None, None, None),
            P("row", "col", None, None),
            P("row", "col"),
        ),
        out_specs=(P("row", "col"), P("row", "col")),
        check_vma=False,
    )
```
